32 devices in a mesh: fsdp: 16 (over z, x, core), rep: 2 (over y).
Axes of the slice: x: 2, y: 2, z: 4, core: 2. Of those that a mesh axis runs over, the one named last changes fastest.
Arguments:
- hidden_in: float32 [4096, 1536], P(('fsdp', 'rep')), may hold values from -6 to 6
- seg_ids: int32 [32, 128], P(('fsdp', 'rep')), may hold values from -1 to 127, as said below
- norm_gain: bfloat16 [2, 1536], P(None, 'fsdp'), may hold values from 0.5 to 1.5
- in_weight: bfloat16 [2, 1536, 6448], P(None, 'fsdp'), may hold values from -0.15625 to 0.15625
- conv_weight: bfloat16 [2, 4, 3328], P(None, None, 'fsdp'), may hold values from -3 to 3
- conv_bias: bfloat16 [2, 3328], P(None, 'fsdp'), may hold values from -3 to 3
- dt_bias: float32 [2, 48], replicated, may hold values from -5.5 to -3
- a_log: float32 [2, 48], replicated, may hold values from -1 to 2.5
- d_skip: float32 [2, 48], replicated, may hold values from 0.5 to 1.5
- gate_gain: bfloat16 [2, 3072], P(None, 'fsdp'), may hold values from 0.5 to 1.5
- out_weight: bfloat16 [2, 3072, 1536], P(None, 'fsdp'), may hold values from -0.109375 to 0.109375
- cotangent: float32 [4096, 1536], P(('fsdp', 'rep')), may hold values from -6 to 6
Outputs:
- hidden_out: float32 [4096, 1536], P(('fsdp', 'rep'))
- hidden_grad: float32 [4096, 1536], P(('fsdp', 'rep'))
- grad_norm_gain: float32 [2, 1536], P(None, 'fsdp')
- grad_in_weight: float32 [2, 1536, 6448], P(None, 'fsdp')
- grad_conv_weight: float32 [2, 4, 3328], P(None, None, 'fsdp')
- grad_conv_bias: float32 [2, 3328], P(None, 'fsdp')
- grad_dt_bias: float32 [2, 48], replicated
- grad_a_log: float32 [2, 48], replicated
- grad_d_skip: float32 [2, 48], replicated
- grad_gate_gain: float32 [2, 3072], P(None, 'fsdp')
- grad_out_weight: float32 [2, 3072, 1536], P(None, 'fsdp')
The draws below stay inside these ranges and needn't reach their ends.
Inputs may be any that keep to these rules, and one draw needn't show every extreme that they name: `seg_ids`: in each row (one micro-batch's 128 slots) the live slots come first, at least 32 of them, and some row is live in full and ends with a sequence of one token; a live slot holds the position in its row at which its sequence begins, the slots after the live ones hold -1.
All inputs are finite; a program needn't handle non-finite values.
Results may differ from the reference program's by a relative error of at most 0.012.
Values may be sent and summed in bfloat16 or wider, within the bound.
No kernel may reach another device: no remote copies, remote signals or barrier semaphores. Data moves between devices by JAX's collectives and lax.ppermute only.
A program may use at most 384 MiB of HBM per device.

```python
import math
import jax
import jax.numpy as jnp
from jax import lax

D = 1536
H = 48
KW = 4
LAYERS = 2
TOK_DEV = 128
DI = 3072
CONV = 3328
E = 6448
ROWS = 32
TOKENS = 4096


def draw_seg_ids(key, part):
    key_live, key_full, key_starts = jax.random.split(key, 3)
    live_count = jax.random.randint(key_live, (ROWS,), TOK_DEV // 4, TOK_DEV)
    full_row = jax.random.randint(key_full, (), 0, ROWS)
    row_index = jnp.arange(ROWS)
    live_count = jnp.where(row_index == full_row, TOK_DEV, live_count)
    positions = jnp.arange(TOK_DEV)
    starts = jax.random.randint(key_starts, (ROWS, TOK_DEV), 0, 64) == 0
    starts = starts | (positions == 0)[None, :]
    starts = starts | (row_index == full_row)[:, None] & (positions == TOK_DEV - 1)[None, :]
    marks = jnp.where(starts, positions[None, :], 0)
    begins = lax.cummax(marks, axis=1)
    return jnp.where(positions[None, :] < live_count[:, None], begins, -1).astype(jnp.int32)


def with_spikes(array, own_key, source, target, parts, factor):
    def block_of(axis_at):
        return (jnp.arange(array.shape[axis_at]) // (array.shape[axis_at] // parts)).reshape((-1,) + (1,) * (array.ndim - 1 - axis_at))

    first = jax.random.permutation(own_key, parts)[block_of(target)]
    other_side = (block_of(target) + parts // 2) % parts
    return jnp.where((block_of(source) == first) | (block_of(source) == other_side), factor * array, array)


def block_levels(key, dims, shards, smallest, top_value):
    factor_of = 1.0
    for axis_at, blocks in shards:
        heights = jax.random.uniform(jax.random.fold_in(jax.random.fold_in(key, 6), axis_at), (blocks,), jnp.float32, smallest / len(shards), top_value / len(shards))
        factor_of = factor_of * jnp.repeat(jnp.exp(heights), dims[axis_at] // blocks).reshape((-1,) + (1,) * (len(dims) - 1 - axis_at))
    return factor_of


def centred(stream_key, dims, scale, most, cuts=(), kind=jnp.bfloat16):
    loudness = block_levels(stream_key, dims, cuts, -0.22, 0.18) if cuts else 1.0
    array = jax.random.normal(stream_key, dims, jnp.float32) * scale * loudness
    return jnp.minimum(jnp.maximum(array, -most), most).astype(kind)


def gaussian_with(key, extent, scale, reach, pieces, heavy, kind=jnp.bfloat16):
    values = scale * jax.random.normal(key, extent, jnp.float32)
    if pieces:
        values = values * block_levels(key, extent, pieces, -0.22, 0.18)
    return jnp.clip(with_spikes(values, jax.random.fold_in(key, 3), *heavy), -reach, reach).astype(kind)


def setup_inputs(seed: int = 0) -> dict:
    seeds = jax.random.split(jax.random.key(seed), 13)
    hidden_in = gaussian_with(seeds[0], (TOKENS, D), 1.0, 6.0, ((0, 32),), (0, 1, 32, 2.75), jnp.float32)
    seg_ids = draw_seg_ids(jax.random.fold_in(seeds[12], 71), 0)
    norm_gain = jnp.clip(1.0 + 0.1 * jax.random.normal(seeds[2], (LAYERS, D), jnp.float32), 0.5, 1.5).astype(jnp.bfloat16)
    in_weight = centred(seeds[3], (LAYERS, D, E), D ** -0.5, 0.15625, ((1, 16),))
    conv_weight = centred(seeds[4], (LAYERS, KW, CONV), KW ** -0.5, 3.0, ((2, 16),))
    conv_bias = centred(seeds[5], (LAYERS, CONV), 0.5, 3.0, ((1, 16),))
    dt_bias = jnp.clip(jax.random.uniform(seeds[6], (LAYERS, H), jnp.float32, -5.5, -3.0), -5.5, -3.0)
    a_log = jnp.clip(jax.random.uniform(seeds[7], (LAYERS, H), jnp.float32, -1.0, 2.5), -1.0, 2.5)
    d_skip = jnp.clip(jax.random.uniform(seeds[8], (LAYERS, H), jnp.float32, 0.5, 1.5), 0.5, 1.5)
    gate_gain = jnp.clip(1.0 + 0.1 * jax.random.normal(seeds[9], (LAYERS, DI), jnp.float32), 0.5, 1.5).astype(jnp.bfloat16)
    out_weight = centred(seeds[10], (LAYERS, DI, D), DI ** -0.5, 0.109375, ((1, 16),))
    cotangent = centred(seeds[11], (TOKENS, D), 1.0, 6.0, ((0, 32),), jnp.float32)
    return dict(hidden_in=hidden_in, seg_ids=seg_ids, norm_gain=norm_gain, in_weight=in_weight, conv_weight=conv_weight, conv_bias=conv_bias, dt_bias=dt_bias, a_log=a_log, d_skip=d_skip, gate_gain=gate_gain, out_weight=out_weight, cotangent=cotangent)


EPS = 1e-05

def rms_scale(hidden, gain_vec):
    return hidden * lax.rsqrt(lax.optimization_barrier(jnp.mean(hidden * hidden, axis=-1, keepdims=True)) + EPS) * gain_vec

def conv_mix(xbc_in, segment, conv_taps, conv_shift):
    kernel_len = conv_taps.shape[0]
    token_count = xbc_in.shape[0]
    result = conv_shift[None, :] + conv_taps[kernel_len - 1][None, :] * xbc_in
    for offset in range(1, kernel_len):
        shifted = jnp.pad(xbc_in, ((offset, 0), (0, 0)))[:token_count]
        prior_seg = jnp.pad(segment, (offset, 0), constant_values=-2)[:token_count]
        keep_mask = (prior_seg == segment).astype(xbc_in.dtype)[:, None]
        result = result + conv_taps[kernel_len - 1 - offset][None, :] * shifted * keep_mask
    return result

def scan_group(group_items, cross_terms, same_seq):
    values_g, steps_g, logs_g = group_items
    running = jnp.cumsum(steps_g * (-jnp.exp(logs_g))[None, :], axis=0).T
    spread = running[:, :, None] - running[:, None, :]
    decay_map = jnp.where(same_seq[None], jnp.exp(jnp.where(same_seq[None], spread, 0.0)), 0.0)
    weighted = decay_map * cross_terms[None]
    scaled = values_g * steps_g[:, :, None]
    return jnp.einsum('gts,sgp->tgp', weighted, scaled, precision=lax.Precision.HIGHEST)

def mixer(projected, conv_taps, conv_shift, bias_dt, log_decay, skip_gain, gate_vec, segment):
    inner_width = gate_vec.shape[0]
    head_count = bias_dt.shape[0]
    head_width = inner_width // head_count
    conv_width = conv_shift.shape[0]
    state_width = (conv_width - inner_width) // 2
    token_count = projected.shape[0]
    gate_in = projected[:, :inner_width]
    xbc_in = projected[:, inner_width:inner_width + conv_width]
    dt_raw = projected[:, inner_width + conv_width:]
    activated = jax.nn.silu(conv_mix(xbc_in, segment, conv_taps, conv_shift))
    values = activated[:, :inner_width]
    b_in = activated[:, inner_width:inner_width + state_width]
    c_out = activated[:, inner_width + state_width:]
    steps_dt = jax.nn.softplus(dt_raw + bias_dt[None, :])
    positions = jnp.arange(token_count)
    same_seq = (segment[:, None] == segment[None, :]) & (positions[:, None] >= positions[None, :])
    cross_terms = jnp.dot(c_out, b_in.T, precision=lax.Precision.HIGHEST)
    group_size = math.gcd(head_count, max(1, 48 * 16384 // (token_count * token_count)))
    group_count = head_count // group_size
    values_grouped = values.reshape(token_count, group_count, group_size, head_width).transpose(1, 0, 2, 3)
    steps_grouped = steps_dt.reshape(token_count, group_count, group_size).transpose(1, 0, 2)
    logs_grouped = log_decay.reshape(group_count, group_size)

    def group_fn(group_items):
        return scan_group(group_items, cross_terms, same_seq)
    scanned = lax.map(jax.checkpoint(group_fn), (values_grouped, steps_grouped, logs_grouped))
    scanned = scanned.transpose(1, 0, 2, 3).reshape(token_count, inner_width)
    scanned = scanned + values * jnp.repeat(skip_gain, head_width)[None, :]
    gated_out = scanned * jax.nn.silu(gate_in)
    return rms_scale(gated_out, gate_vec[None, :])

def row_pass(params, row_in, segment, row_cot):
    norm_gain, in_weight, conv_weight, conv_bias, dt_bias, a_log, d_skip, gate_gain, out_weight = params
    layer_total = in_weight.shape[0]
    alive_mask = (segment >= 0).astype(jnp.float32)[:, None]
    stream = row_in
    kept_items = []
    for layer_index in range(layer_total):
        normed = rms_scale(stream, norm_gain[layer_index].astype(jnp.float32)).astype(jnp.bfloat16)
        projected = jnp.dot(normed, in_weight[layer_index], preferred_element_type=jnp.float32)
        mixed_out = mixer(projected, conv_weight[layer_index].astype(jnp.float32), conv_bias[layer_index].astype(jnp.float32), dt_bias[layer_index], a_log[layer_index], d_skip[layer_index], gate_gain[layer_index].astype(jnp.float32), segment).astype(jnp.bfloat16)
        branch = jnp.dot(mixed_out, out_weight[layer_index], preferred_element_type=jnp.float32)
        kept_items.append((stream, normed, projected))
        stream = stream + alive_mask * branch
    grad_stream = row_cot
    layer_grads = [None] * layer_total
    for layer_index in reversed(range(layer_total)):
        layer_in, normed, projected = kept_items[layer_index]
        grad_branch = (alive_mask * grad_stream).astype(jnp.bfloat16)

        def local_mixer(proj_in, taps_in, shift_in, bias_in, logs_in, skip_in, gate_in_vec):
            return mixer(proj_in, taps_in, shift_in, bias_in, logs_in, skip_in, gate_in_vec, segment)
        mixed32, pullback = jax.vjp(local_mixer, projected, conv_weight[layer_index].astype(jnp.float32), conv_bias[layer_index].astype(jnp.float32), dt_bias[layer_index], a_log[layer_index], d_skip[layer_index], gate_gain[layer_index].astype(jnp.float32))
        mixed_out = mixed32.astype(jnp.bfloat16)
        grad_wout = jnp.dot(mixed_out.T, grad_branch, preferred_element_type=jnp.float32)
        grad_mixed = jnp.dot(grad_branch, out_weight[layer_index].T, preferred_element_type=jnp.float32)
        grad_proj32, grad_taps, grad_shift, grad_bias, grad_logs, grad_skip, grad_gate = pullback(grad_mixed)
        grad_proj = grad_proj32.astype(jnp.bfloat16)
        grad_win = jnp.dot(normed.T, grad_proj, preferred_element_type=jnp.float32)
        grad_normed = jnp.dot(grad_proj, in_weight[layer_index].T, preferred_element_type=jnp.float32)
        normed32, norm_pull = jax.vjp(rms_scale, layer_in, norm_gain[layer_index].astype(jnp.float32))
        grad_layer_in, grad_gain = norm_pull(grad_normed)
        grad_stream = grad_stream + grad_layer_in
        layer_grads[layer_index] = (grad_gain, grad_win, grad_taps, grad_shift, grad_bias, grad_logs, grad_skip, grad_gate, grad_wout)
    stacked = tuple((jnp.stack([layer_grads[layer_index][member] for layer_index in range(layer_total)]) for member in range(9)))
    return (stream, grad_stream, stacked)

def reference(hidden_in, seg_ids, norm_gain, in_weight, conv_weight, conv_bias, dt_bias, a_log, d_skip, gate_gain, out_weight, cotangent):
    row_count = seg_ids.shape[0]
    stream_rows = hidden_in.reshape(row_count, TOK_DEV, D)
    cot_rows = cotangent.reshape(row_count, TOK_DEV, D)
    params = (norm_gain, in_weight, conv_weight, conv_bias, dt_bias, a_log, d_skip, gate_gain, out_weight)
    start_sums = tuple((jnp.zeros(member.shape, jnp.float32) for member in params))

    def one_row(running_sum, row_item):
        row_in, segment, row_cot = row_item
        row_out, row_grad, grads_now = row_pass(params, row_in, segment, row_cot)
        return (tuple((before + added for before, added in zip(running_sum, grads_now))), (row_out, row_grad))
    grad_sums, (row_outs, row_grads) = lax.scan(one_row, start_sums, (stream_rows, seg_ids, cot_rows))
    return (row_outs.reshape(TOKENS, D), row_grads.reshape(TOKENS, D), grad_sums[0], grad_sums[1], grad_sums[2], grad_sums[3], grad_sums[4], grad_sums[5], grad_sums[6], grad_sums[7], grad_sums[8])
```

```python
import functools

import jax
import jax.numpy as jnp
import numpy as np
from jax import lax
from jax.experimental import pallas as pl
from jax.experimental.pallas import tpu as pltpu
from jax.sharding import PartitionSpec as P

EPS = 1e-05
BF = jnp.bfloat16
F32 = jnp.float32
AXES = ("fsdp", "rep")
LANES = 128
INNER = 4
HIGH = lax.Precision.HIGHEST


def dot(a, b):
    return lax.dot_general(a, b, (((1,), (0,)), ((), ())), preferred_element_type=F32)


def dot_nt(a, b):
    return lax.dot_general(a, b, (((1,), (1,)), ((), ())), preferred_element_type=F32)


def dot_tn(a, b):
    return lax.dot_general(a, b, (((0,), (0,)), ((), ())), preferred_element_type=F32)


def dot_high(a, b):
    return lax.dot_general(
        a, b, (((1,), (0,)), ((), ())), precision=HIGH, preferred_element_type=F32
    )


def dot_high_nt(a, b):
    return lax.dot_general(
        a, b, (((1,), (1,)), ((), ())), precision=HIGH, preferred_element_type=F32
    )


def sigmoid(v):
    return 1.0 / (1.0 + jnp.exp(-v))


def tile_lanes(mask, width):
    return jnp.concatenate([mask] * (width // mask.shape[1]), axis=1)


def keep_masks(seg_wide, taps):
    token = lax.broadcasted_iota(jnp.int32, seg_wide.shape, 0)
    masks = []
    for offset in range(1, taps):
        same = pltpu.roll(seg_wide, offset, 0) == seg_wide
        masks.append(jnp.where(same & (token >= offset), 1.0, 0.0))
    return masks


def conv_forward(x, masks, tap_rows, bias):
    taps = len(tap_rows)
    total = bias + tap_rows[taps - 1] * x
    for offset in range(1, taps):
        mask = tile_lanes(masks[offset - 1], x.shape[1])
        total = total + tap_rows[taps - 1 - offset] * (pltpu.roll(x, offset, 0) * mask)
    return total


def conv_backward(du, x, masks, tap_rows):
    taps = len(tap_rows)
    tokens = x.shape[0]
    dx = tap_rows[taps - 1] * du
    dtaps = [None] * taps
    dtaps[taps - 1] = jnp.sum(du * x, axis=0, keepdims=True)
    for offset in range(1, taps):
        held = du * tile_lanes(masks[offset - 1], x.shape[1])
        dx = dx + tap_rows[taps - 1 - offset] * pltpu.roll(held, tokens - offset, 0)
        dtaps[taps - 1 - offset] = jnp.sum(
            held * pltpu.roll(x, offset, 0), axis=0, keepdims=True
        )
    return dx, dtaps, jnp.sum(du, axis=0, keepdims=True)


def split_hi_lo(v):
    hi = v.astype(BF).astype(F32)
    return hi, v - hi


def emit_input(h, seg_wide, gain, w_small, vec_small, dims, pay_ref, small_ref):
    model, state2, heads, taps = dims
    scale = lax.rsqrt(jnp.mean(h * h, axis=-1, keepdims=True) + EPS)
    normed = (h * scale * gain).astype(BF)
    small = dot(normed, w_small)
    small_ref[...] = small
    masks = keep_masks(seg_wide, taps)
    tap_rows = [vec_small[k : k + 1, :] for k in range(taps)]
    pre = conv_forward(small[:, :state2], masks, tap_rows, vec_small[taps : taps + 1, :])
    dt_in = small[:, state2 : state2 + LANES] + vec_small[taps + 1 : taps + 2, :LANES]
    dt = jnp.maximum(dt_in, 0.0) + jnp.log1p(jnp.exp(-jnp.abs(dt_in)))
    hi, lo = split_hi_lo(dt)
    lane = lax.broadcasted_iota(jnp.int32, hi.shape, 1)
    block = jnp.where(
        lane < heads,
        hi,
        jnp.where(
            lane < 2 * heads,
            pltpu.roll(lo, heads, 1),
            jnp.where(lane == 2 * heads, seg_wide, 0.0),
        ),
    )
    pay_ref[:, :model] = normed
    pay_ref[:, model : model + state2] = (pre * sigmoid(pre)).astype(BF)
    pay_ref[:, model + state2 :] = block.astype(BF)


def finish_forward(parts, h, seg_wide, inner, raw_ref, scale_ref):
    model = h.shape[1]
    total = parts[0].astype(F32)
    for part in parts[1:]:
        total = total + part.astype(F32)
    raw = total[:, :model]
    scale = lax.rsqrt(total[:, model : model + LANES] * (1.0 / inner) + EPS)
    raw_ref[...] = raw
    scale_ref[...] = scale
    live = jnp.where(seg_wide >= 0.0, scale, 0.0)
    return h + tile_lanes(live, model) * raw, raw, scale


def emit_cotangent(grad, seg_wide, raw, scale, inner, pay_ref):
    model = grad.shape[1]
    live = tile_lanes(jnp.where(seg_wide >= 0.0, 1.0, 0.0), model)
    branch = (live * grad).astype(BF)
    along = jnp.sum(branch.astype(F32) * raw, axis=-1, keepdims=True)
    drag = scale * scale * scale * (along * (1.0 / inner))
    s_hi, s_lo = split_hi_lo(scale)
    d_hi, d_lo = split_hi_lo(drag)
    lane = lax.broadcasted_iota(jnp.int32, scale.shape, 1)
    block = jnp.where(
        lane == 0, s_hi, jnp.where(lane == 1, s_lo, jnp.where(lane == 2, d_hi, d_lo))
    )
    pay_ref[:, :model] = branch
    pay_ref[:, model:] = block.astype(BF)


def first_kernel(dims, h_ref, seg_ref, gain_ref, ws_ref, vec_ref, pay_ref, small_ref):
    emit_input(
        h_ref[...], seg_ref[...], gain_ref[...], ws_ref[...], vec_ref[...], dims, pay_ref, small_ref
    )


def middle_kernel(dims, inner, *refs):
    parts = [ref[...] for ref in refs[:4]]
    h_ref, seg_ref, gain_ref, ws_ref, vec_ref = refs[4:9]
    pay_ref, small_ref, h_out, raw_ref, scale_ref = refs[9:]
    seg = seg_ref[...]
    h, _, _ = finish_forward(parts, h_ref[...], seg, inner, raw_ref, scale_ref)
    h_out[...] = h
    emit_input(h, seg, gain_ref[...], ws_ref[...], vec_ref[...], dims, pay_ref, small_ref)


def turn_kernel(inner, *refs):
    parts = [ref[...] for ref in refs[:4]]
    h_ref, seg_ref, cot_ref = refs[4:7]
    pay_ref, h_out, raw_ref, scale_ref = refs[7:]
    seg = seg_ref[...]
    h, raw, scale = finish_forward(parts, h_ref[...], seg, inner, raw_ref, scale_ref)
    h_out[...] = h
    emit_cotangent(cot_ref[...], seg, raw, scale, inner, pay_ref)


def back_kernel(dims, inner, more, *refs):
    model, state2, heads, taps = dims
    parts = [ref[...] for ref in refs[:4]]
    h_ref, seg_ref, gain_ref, ws_ref, vec_ref, small_ref, grad_ref = refs[4:11]
    vec_a_ref, vec_b_ref = refs[11:13]
    rest = refs[13:]
    if more:
        raw_ref, scale_ref = rest[:2]
        rest = rest[2:]
    grad_out, gs_ref, rowvec_ref = rest[:3]
    seg = seg_ref[...]
    total = parts[0].astype(F32)
    for part in parts[1:]:
        total = total + part.astype(F32)
    vec = vec_ref[...]
    small = small_ref[...]
    masks = keep_masks(seg, taps)
    tap_rows = [vec[k : k + 1, :] for k in range(taps)]
    x = small[:, :state2]
    pre = conv_forward(x, masks, tap_rows, vec[taps : taps + 1, :])
    sig = sigmoid(pre)
    du = total[:, model : model + state2] * (sig * (1.0 + pre * (1.0 - sig)))
    dx, dtaps, dbias = conv_backward(du, x, masks, tap_rows)
    dt_in = small[:, state2 : state2 + LANES] + vec[taps + 1 : taps + 2, :LANES]
    ddt = total[:, model + state2 :] * sigmoid(dt_in)
    gs = jnp.concatenate([dx, ddt], axis=1).astype(BF)
    gs_ref[...] = gs
    gn = total[:, :model] + dot_nt(gs, ws_ref[...])
    h = h_ref[...]
    gain = gain_ref[...]
    scale = lax.rsqrt(jnp.mean(h * h, axis=-1, keepdims=True) + EPS)
    dgain = jnp.sum(gn * (h * scale), axis=0, keepdims=True)
    inner_grad = gn * gain
    along = jnp.mean(inner_grad * h, axis=-1, keepdims=True)
    grad = grad_ref[...] + scale * inner_grad - h * (scale * scale * scale * along)
    grad_out[...] = grad
    rowvec_ref[...] = jnp.zeros_like(rowvec_ref)
    rowvec_ref[:8, :] = vec_a_ref[...] + vec_b_ref[...]
    cols = rowvec_ref.shape[1]
    for k in range(model // cols):
        rowvec_ref[8 + k : 9 + k, :] = dgain[:, k * cols : (k + 1) * cols]
    dbias_dt = jnp.sum(ddt, axis=0, keepdims=True)
    first, per = 8 + model // cols, cols // state2
    for k, line in enumerate(dtaps + [dbias, dbias_dt]):
        start = (k % per) * state2
        rowvec_ref[first + k // per : first + k // per + 1, start : start + line.shape[1]] = line
    if more:
        emit_cotangent(grad, seg, raw_ref[...], scale_ref[...], inner, rest[3])


def heads_here(at_ref, shape, axis, spread=1):
    slots = at_ref.shape[0] - 5
    at = lax.broadcasted_iota(jnp.int32, shape, axis)
    found = jnp.full(shape, -1, jnp.int32)
    for slot in range(slots):
        inside = (at >= slot * spread) & (at < (slot + 1) * spread)
        found = jnp.where(inside, at_ref[5 + slot], found)
    return found


def per_head(at_ref, values_ref, layer, shape, axis, spread=1):
    slots = at_ref.shape[0] - 5
    at = lax.broadcasted_iota(jnp.int32, shape, axis)
    found = jnp.zeros(shape, F32)
    for slot in range(slots):
        inside = (at >= slot * spread) & (at < (slot + 1) * spread)
        found = jnp.where(inside, values_ref[layer, at_ref[5 + slot]], found)
    return found


def rank_setup(dims, layer, at_ref, alog_ref):
    slots, width, heads = dims
    across = heads_here(at_ref, (1, LANES), 1)
    k = lax.broadcasted_iota(jnp.int32, (LANES, LANES), 0)
    lane = lax.broadcasted_iota(jnp.int32, (LANES, LANES), 1)
    sel = (k == across) | ((k == across + heads) & (across >= 0))
    sel = sel | ((k == 2 * heads) & (lane == slots))
    down = heads_here(at_ref, (16, 1), 0)
    lane_t = lax.broadcasted_iota(jnp.int32, (16, LANES), 1)
    slot_t = lax.broadcasted_iota(jnp.int32, (16, LANES), 0)
    sel_t = (lane_t == down) | ((lane_t == down + heads) & (down >= 0))
    seg_t = (lane_t == 2 * heads) & (slot_t == slots)
    home_t = lane_t == down
    wide = heads_here(at_ref, (1, slots * width), 1, width)
    k_x = lax.broadcasted_iota(jnp.int32, (LANES, slots * width), 0)
    sel_x = (k_x == wide) | (k_x == wide + heads)
    one = lambda m: jnp.where(m, 1.0, 0.0).astype(BF)
    rate_row = per_head(at_ref, alog_ref, layer, (1, LANES), 1)
    rate_row = jnp.where(across >= 0, -jnp.exp(rate_row), 0.0)
    rate_col = per_head(at_ref, alog_ref, layer, (16, 1), 0)
    rate_col = jnp.where(down >= 0, -jnp.exp(rate_col), 0.0)
    return one(sel), one(sel_t | seg_t), one(home_t), one(sel_x), rate_row, rate_col


def pair_parts(wide, half):
    lane = lax.broadcasted_iota(jnp.int32, wide.shape, 1)
    first = jnp.where(lane < half, wide, 0.0)
    return jnp.concatenate([first, wide - first], axis=0).astype(BF)


def load_out_weight(groups, at_ref, own, other, wo_ref):
    g, core = at_ref[0], at_ref[4]
    for k in range(groups):
        rows = own[k].shape[0]
        plane = lax.rem(g + groups - k, groups)
        at = pl.ds(pl.multiple_of(plane * rows, rows), rows)
        wo_ref[core, at, :] = own[k][...]
        wo_ref[1 - core, at, :] = other[k][...]


def rank_forward_kernel(dims, rows, groups, layer, *refs):
    model, state, slots, width, taps, heads = dims
    at_ref, alog_ref, skip_ref = refs[:3]
    pays = refs[3 : 3 + rows]
    refs = refs[3 + rows :]
    win_own, refs = refs[: 2 * groups], refs[2 * groups :]
    win_other, refs = refs[: 2 * groups], refs[2 * groups :]
    wo_own, refs = refs[:groups], refs[groups:]
    wo_other, refs = refs[:groups], refs[groups:]
    vec_ref, outs = refs[0], refs[1 : 1 + rows]
    zv_ref, y_ref, gated_ref, wo_ref, side_ref, tail_ref = refs[1 + rows :]
    tokens = pays[0].shape[0]
    cols = slots * width
    half = cols // 2
    g, core = at_ref[0], at_ref[4]
    step = model // groups
    for chunk in range(2):
        lanes = slice(chunk * half, (chunk + 1) * half)
        own = other = None
        for k in range(groups):
            plane = lax.rem(g + groups - k, groups)
            at = pl.ds(pl.multiple_of(plane * step, step), step)
            left = jnp.concatenate([pay[:, at] for pay in pays], axis=0)
            a = dot(left, win_own[chunk * groups + k][...])
            b = dot(left, win_other[chunk * groups + k][...])
            own = a if own is None else own + a
            other = b if other is None else other + b
        zv_ref[core, :, lanes] = own
        zv_ref[1 - core, :, lanes] = other
    load_out_weight(groups, at_ref, wo_own, wo_other, wo_ref)
    sel, sel_t, _, sel_x, rate_row, rate_col = rank_setup((slots, width, heads), layer, at_ref, alog_ref)
    for row in range(rows):
        side_ref[row * tokens : (row + 1) * tokens, :] = pays[row][:, model:]
    vec = vec_ref[...]
    tap_rows = [vec[k : k + 1, :] for k in range(taps)]
    bias, gain = (vec[taps + k : taps + k + 1, :] for k in range(2))
    skip = per_head(at_ref, skip_ref, layer, (1, cols), 1, width)
    t_at = lax.broadcasted_iota(jnp.int32, (tokens, tokens), 0)
    s_at = lax.broadcasted_iota(jnp.int32, (tokens, tokens), 1)
    lower = jnp.where(t_at >= s_at, 1.0, 0.0)

    def one_row(row, carry):
        at = pl.ds(pl.multiple_of(row * tokens, tokens), tokens)
        block = side_ref[at, 2 * state :]
        dts = dot(block, sel)
        dts_t = dot_nt(sel_t, block)
        dt_wide = dot(block, sel_x)
        running = dot_high(lower, dts * rate_row)
        running_t = dot_high_nt(dts_t * rate_col, lower)
        seg_row = dts_t[slots : slots + 1, :]
        seg_wide = jnp.broadcast_to(dts[:, slots : slots + 1], (tokens, tokens))
        valid = (seg_wide == seg_row) & (t_at >= s_at)
        cross = jnp.where(valid, dot_nt(side_ref[at, state : 2 * state], side_ref[at, :state]), 0.0)
        masks = keep_masks(seg_wide, taps)
        pre = conv_forward(zv_ref[1, at, :], masks, tap_rows, bias)
        values = pre * sigmoid(pre)
        scaled = dt_wide * values
        for pair in range(slots // 2):
            lanes = slice(pair * 2 * width, (pair + 1) * 2 * width)
            maps = []
            for head in (2 * pair, 2 * pair + 1):
                spread = running[:, head : head + 1] - running_t[head : head + 1, :]
                maps.append((jnp.exp(jnp.minimum(spread, 0.0)) * cross).astype(BF))
            y_ref[at, lanes] = dot(
                jnp.concatenate(maps, axis=1), pair_parts(scaled[:, lanes], width)
            )
        z = zv_ref[0, at, :]
        gated = (y_ref[at, :] + values * skip) * (z * sigmoid(z))
        gated_ref[at, :] = (gated * gain).astype(BF)
        squares = jnp.sum(gated * gated, axis=-1, keepdims=True)
        tail_ref[at, :] = jnp.broadcast_to(squares, (tokens, LANES)).astype(BF)
        return carry

    lax.fori_loop(0, rows, one_row, 0)
    span = wo_ref.shape[2]
    for side in range(2):
        result = dot(gated_ref[...], wo_ref[side]).astype(BF)
        for row in range(rows):
            outs[row][:, side * span : (side + 1) * span] = result[row * tokens : (row + 1) * tokens]
    for row in range(rows):
        outs[row][:, model:] = tail_ref[row * tokens : (row + 1) * tokens, :]


def rank_backward_kernel(dims, rows, groups, layer, *refs):
    model, state, slots, width, taps, heads = dims
    at_ref, alog_ref, skip_ref = refs[:3]
    cots, pays = refs[3 : 3 + rows], refs[3 + rows : 3 + 2 * rows]
    refs = refs[3 + 2 * rows :]
    win_own, refs = refs[: 2 * groups], refs[2 * groups :]
    win_other, refs = refs[: 2 * groups], refs[2 * groups :]
    wo_own, refs = refs[:groups], refs[groups:]
    wo_other, refs = refs[:groups], refs[groups:]
    vec_ref, zv_ref, y_ref = refs[:3]
    outs = refs[3 : 3 + rows]
    g_ref, mixed_ref, grads_ref = refs[3 + rows : 6 + rows]
    gm_ref, dcross_ref, dxs_ref, wo_ref, side_ref, tail_ref, dside_ref = refs[6 + rows :]
    tokens = pays[0].shape[0]
    cols = slots * width
    half = cols // 2
    g, core = at_ref[0], at_ref[4]
    load_out_weight(groups, at_ref, wo_own, wo_other, wo_ref)
    span = wo_ref.shape[2]
    total = None
    for side in range(2):
        left = jnp.concatenate(
            [cot[:, side * span : (side + 1) * span] for cot in cots], axis=0
        )
        a = dot_nt(left, wo_ref[side])
        total = a if total is None else total + a
    gm_ref[...] = total
    sel, sel_t, home_t, sel_x, rate_row, rate_col = rank_setup(
        (slots, width, heads), layer, at_ref, alog_ref
    )
    for row in range(rows):
        side_ref[row * tokens : (row + 1) * tokens, :] = pays[row][:, model:]
        tail_ref[row * tokens : (row + 1) * tokens, :] = cots[row][:, model:]
    vec = vec_ref[...]
    tap_rows = [vec[k : k + 1, :] for k in range(taps)]
    bias, gain = (vec[taps + k : taps + k + 1, :] for k in range(2))
    skip = per_head(at_ref, skip_ref, layer, (1, cols), 1, width)
    t_at = lax.broadcasted_iota(jnp.int32, (tokens, tokens), 0)
    s_at = lax.broadcasted_iota(jnp.int32, (tokens, tokens), 1)
    lower = jnp.where(t_at >= s_at, 1.0, 0.0)
    upper = jnp.where(t_at <= s_at, 1.0, 0.0)
    col_at = lax.broadcasted_iota(jnp.int32, (cols, LANES), 0)
    lane_at = lax.broadcasted_iota(jnp.int32, (cols, LANES), 1)
    head_sum = jnp.where(
        (col_at >= lane_at * width) & (col_at < (lane_at + 1) * width), 1.0, 0.0
    )
    grads_ref[...] = jnp.zeros_like(grads_ref)

    def one_row(row, carry):
        at = pl.ds(pl.multiple_of(row * tokens, tokens), tokens)
        block = side_ref[at, 2 * state :]
        dts = dot(block, sel)
        dts_t = dot_nt(sel_t, block)
        dt_wide = dot(block, sel_x)
        running = dot_high(lower, dts * rate_row)
        running_t = dot_high_nt(dts_t * rate_col, lower)
        seg_row = dts_t[slots : slots + 1, :]
        seg_wide = jnp.broadcast_to(dts[:, slots : slots + 1], (tokens, tokens))
        valid = (seg_wide == seg_row) & (t_at >= s_at)
        b_in = side_ref[at, :state]
        c_out = side_ref[at, state : 2 * state]
        cross = jnp.where(valid, dot_nt(c_out, b_in), 0.0)
        masks = keep_masks(seg_wide, taps)
        x = zv_ref[1, at, :]
        pre = conv_forward(x, masks, tap_rows, bias)
        sig = sigmoid(pre)
        values = pre * sig
        scaled = dt_wide * values
        z = zv_ref[0, at, :]
        zsig = sigmoid(z)
        gate = z * zsig
        y = y_ref[at, :]
        scanned = y + values * skip
        gated = scanned * gate
        tail = tail_ref[at, :].astype(F32)
        scale = tail[:, 0:1] + tail[:, 1:2]
        drag = tail[:, 2:3] + tail[:, 3:4]
        gm = gm_ref[at, :]
        scaled_gated = gated * scale
        mixed_ref[at, :] = (scaled_gated * gain).astype(BF)
        grads_ref[taps + 1 : taps + 2, :] += jnp.sum(gm * scaled_gated, axis=0, keepdims=True)
        dgated = gm * gain * scale - gated * drag
        dscan = dgated * gate
        g_ref[0, at, :] = (dgated * scanned * (zsig * (1.0 + z * (1.0 - zsig)))).astype(BF)
        grads_ref[taps + 2 : taps + 3, :] += jnp.sum(dscan * values, axis=0, keepdims=True)
        dcross_ref[...] = jnp.zeros_like(dcross_ref)
        for pair in range(slots // 2):
            lanes = slice(pair * 2 * width, (pair + 1) * 2 * width)
            d_parts = pair_parts(dscan[:, lanes], width)
            scaled_b = scaled[:, lanes].astype(BF)
            dmaps = dot_nt(d_parts, scaled_b)
            maps = []
            dcross = dcross_ref[...]
            for k, head in enumerate((2 * pair, 2 * pair + 1)):
                spread = running[:, head : head + 1] - running_t[head : head + 1, :]
                decay = jnp.exp(jnp.minimum(spread, 0.0))
                maps.append((decay * cross).astype(BF))
                dcross = dcross + dmaps[k * tokens : (k + 1) * tokens] * decay
            dcross_ref[...] = dcross
            dxs_ref[:, lanes] = dot_tn(jnp.concatenate(maps, axis=0), d_parts)
        dxs = dxs_ref[...]
        dval = dscan * skip + dt_wide * dxs
        flow = dscan.astype(BF).astype(F32) * y - scaled.astype(BF).astype(F32) * dxs
        sums = dot_high(jnp.concatenate([values * dxs, flow], axis=0), head_sum)
        carried = dot_high(upper, sums[tokens:])
        ddt = sums[:tokens] + carried * rate_row
        grads_ref[taps + 3 : taps + 4, :LANES] += (
            jnp.sum(dts * carried, axis=0, keepdims=True) * rate_row
        )
        dcross_b = jnp.where(valid, dcross_ref[...], 0.0).astype(BF)
        dside_ref[at, :state] = dot_tn(dcross_b, c_out).astype(BF)
        dside_ref[at, state : 2 * state] = dot(dcross_b, b_in).astype(BF)
        dside_ref[at, 2 * state :] = dot(ddt[:, :16].astype(BF), home_t).astype(BF)
        du = dval * (sig * (1.0 + pre * (1.0 - sig)))
        dx, dtaps, dbias = conv_backward(du, x, masks, tap_rows)
        g_ref[1, at, :] = dx.astype(BF)
        for k in range(taps):
            grads_ref[k : k + 1, :] += dtaps[k]
        grads_ref[taps : taps + 1, :] += dbias
        return carry

    lax.fori_loop(0, rows, one_row, 0)
    step = model // groups
    for k in range(groups):
        plane = lax.rem(g + groups - k, groups)
        at = pl.ds(pl.multiple_of(plane * step, step), step)
        back = None
        for chunk in range(2):
            lanes = slice(chunk * half, (chunk + 1) * half)
            a = dot_nt(g_ref[core, :, lanes], win_own[chunk * groups + k][...])
            a = a + dot_nt(g_ref[1 - core, :, lanes], win_other[chunk * groups + k][...])
            back = a if back is None else back + a
        back = back.astype(BF)
        for row in range(rows):
            outs[row][:, at] = back[row * tokens : (row + 1) * tokens]
    for row in range(rows):
        outs[row][:, model:] = dside_ref[row * tokens : (row + 1) * tokens, :]


def weight_grad_kernel(flip, counts, block, *refs):
    at_ref, refs = refs[0], refs[1:]
    rows, sets = counts
    xs, refs = refs[:rows], refs[rows:]
    gs, refs = refs[:sets], refs[sets:]
    mixed, refs = refs[:sets], refs[sets:]
    cots, out_ref = refs[:rows], refs[rows]
    core = at_ref[4]
    side = (1 - core) if flip else core
    span = out_ref.shape[1]
    model = span * 2
    right = jnp.concatenate([ref[side] for ref in gs], axis=0)
    for start in range(0, model, block):
        left = jnp.concatenate([ref[:, start : start + block] for ref in xs], axis=0)
        out_ref[start : start + block, :] = dot_tn(left, right).astype(BF)
    at = pl.ds(pl.multiple_of(side * span, span), span)
    right = jnp.concatenate([ref[:, at] for ref in cots], axis=0)
    for start in range(0, mixed[0].shape[1], block):
        left = jnp.concatenate([ref[:, start : start + block] for ref in mixed], axis=0)
        out_ref[model + start : model + start + block, :] = dot_tn(left, right).astype(BF)


def small_grad_kernel(rows, block, *refs):
    xs, gs, out_ref = refs[:rows], refs[rows : 2 * rows], refs[2 * rows]
    right = jnp.concatenate([ref[...] for ref in gs], axis=0)
    for start in range(0, out_ref.shape[0], block):
        left = jnp.concatenate([ref[:, start : start + block] for ref in xs], axis=0)
        out_ref[start : start + block, :] = dot_tn(left, right).astype(BF)


def pick_columns_kernel(groups, members, reps, offsets, at_ref, w_ref, *outs):
    rep, far, core = at_ref[2], at_ref[3], at_ref[4]
    span = outs[0].shape[1] // groups
    for x in range(members // 2):
        for part, offset in enumerate(offsets):
            slot = lax.bitwise_xor(far, jnp.int32(x)) * 2 + lax.bitwise_xor(core, jnp.int32(part))
            for which in range(reps):

                @pl.when(rep == which)
                def _(x=x, slot=slot, which=which, offset=offset):
                    starts = [offset + (k * members + 2 * x + which) * span for k in range(groups)]
                    piece = jnp.concatenate([w_ref[0, :, at : at + span] for at in starts], axis=1)
                    for k, out in enumerate(outs):

                        @pl.when(slot == k)
                        def _(out=out, piece=piece):
                            out[...] = piece


def arrange_kernel(at_ref, *refs):
    pieces, (low_ref, high_ref) = refs[:-2], refs[-2:]
    me = at_ref[1]
    rows, span = pieces[0].shape[0], low_ref.shape[1]
    for away, ref in enumerate(pieces):
        at = pl.ds(pl.multiple_of(lax.bitwise_xor(me, jnp.int32(away)) * rows, rows), rows)
        low_ref[at, :] = ref[:, :span]
        high_ref[at, :] = ref[:, span:]


def place_small_kernel(groups, members, reps, layers, taps, widths, at_ref, *refs):
    conv_d, rows_i, rows_d = widths
    ins, bias_ref, outs = refs[:8], refs[8], refs[9:-1]
    vec_ref = refs[-1]
    weights, gains = outs[:layers], outs[layers : 2 * layers]
    shared, ranked = outs[2 * layers : 3 * layers], outs[3 * layers :]
    g, me, rep, far = at_ref[0], at_ref[1], at_ref[2], at_ref[3]
    total = ins[0].shape[1]
    count = groups * members
    rows = weights[0].shape[0] // (count * reps)
    for place in range(8):
        away, side = (place // 4) + 2 * (place % 2), (place // 2) % 2
        ref = ins[place]
        for k in range(groups):
            plane = lax.rem(g + groups - k, groups)
            owner = plane * members + lax.bitwise_xor(me, jnp.int32(away))
            start = (owner * reps + lax.bitwise_xor(rep, jnp.int32(side))) * rows
            for layer in range(layers):
                weights[layer][pl.ds(pl.multiple_of(start, rows), rows), :] = ref[
                    k, layer * rows : (layer + 1) * rows
                ]
            if side == 0:
                vec_ref[owner] = ref[k, layers * rows : total].astype(F32)
    for layer in range(layers):
        at = layer * (taps + 3)
        gains[layer][...] = jnp.concatenate(
            [vec_ref[f, at + taps + 2 : at + taps + 3, :rows_d] for f in range(count)], axis=1
        )
        conv = jnp.concatenate(
            [vec_ref[f, at : at + taps + 1, :conv_d] for f in range(count)], axis=1
        )
        inner = count * rows_i
        shared[layer][...] = jnp.zeros_like(shared[layer])
        shared[layer][: taps + 1, :] = conv[:, inner:]
        shared[layer][taps + 1 : taps + 2, : bias_ref.shape[1]] = bias_ref[layer : layer + 1, :]
        for rank in range(members):

            @pl.when(far * reps + rep == rank)
            def _(rank=rank, layer=layer, at=at, conv=conv):
                starts = [(k * members + rank) * rows_i for k in range(groups)]
                ranked[layer][...] = jnp.zeros_like(ranked[layer])
                ranked[layer][: taps + 1, :] = jnp.concatenate(
                    [conv[:, start : start + rows_i] for start in starts], axis=1
                )
                ranked[layer][taps + 1 : taps + 2, :] = jnp.concatenate(
                    [
                        vec_ref[k * members + rank, at + taps + 1 : at + taps + 2, :rows_i]
                        for k in range(groups)
                    ],
                    axis=1,
                )


def spread_grads_kernel(groups, members, reps, offsets, chunks, *refs):
    at_ref = refs[0]
    sides = [refs[1 : 1 + 2 * chunks : 2], refs[2 : 2 + 2 * chunks : 2]]
    small_own, small_other, out_own, out_other = refs[1 + 2 * chunks : 5 + 2 * chunks]
    in_ref, out_ref = refs[-2:]
    rep, far, core = at_ref[2], at_ref[3], at_ref[4]
    per = groups // chunks
    span = sides[0][0].shape[1] // per
    rows_d = in_ref.shape[1]
    for x in range(members // 2):
        for part, offset in enumerate(offsets):
            slot = lax.bitwise_xor(core, jnp.int32(part)) * 2 + lax.bitwise_xor(far, jnp.int32(x))
            at = pl.ds(pl.multiple_of(slot * rows_d, rows_d), rows_d)
            for which in range(reps):
                for side in range(2):

                    @pl.when(lax.bitwise_xor(rep, jnp.int32(which)) == side)
                    def _(x=x, which=which, offset=offset, side=side, at=at):
                        for q in range(chunks):
                            piece = sides[side][q][at, :].astype(F32)
                            for k in range(per):
                                to = offset + ((q * per + k) * members + 2 * x + which) * span
                                in_ref[0, :, to : to + span] = piece[:, k * span : (k + 1) * span]

    rows = small_own.shape[0]
    first = offsets[-1] + members * groups * span
    wide = in_ref.shape[2] - first
    for ref, side in ((small_own, rep), (small_other, 1 - rep)):
        at = pl.ds(pl.multiple_of(side * rows, rows), rows)
        in_ref[0, at, first:] = ref[:, :wide].astype(F32)
    cut, size = out_own.shape[1], out_ref.shape[1]
    for half in range(2):
        slot = lax.bitwise_xor(core, jnp.int32(half))
        at = pl.ds(pl.multiple_of(slot * size, size), size)
        for ref, home in ((out_own, True), (out_other, False)):

            @pl.when((core == rep) if home else (core != rep))
            def _(half=half, at=at, ref=ref):
                out_ref[0, :, half * cut : (half + 1) * cut] = ref[at, :].astype(F32)


def spread_vectors_kernel(groups, members, reps, layers, taps, heads, at_ref, *refs):
    ins, outs, all_ref = refs[:members], refs[members:-1], refs[-1]
    norm_out, taps_out, conv_out, gate_out, bias_out, alog_out, skip_out = outs
    g, me, rep, far = at_ref[0], at_ref[1], at_ref[2], at_ref[3]
    mine = far * reps + rep
    for away, ref in enumerate(ins):
        order = (0, 2, 1, 3)[away] if reps == 2 else away
        all_ref[lax.bitwise_xor(mine, jnp.int32(order))] = ref[...]
    cols = ins[0].shape[2]
    span = cols // groups
    conv_d, rows_i, rows_d = conv_out.shape[1], gate_out.shape[1], norm_out.shape[1]
    inner = cols * members
    slots = heads // members
    width = cols // slots
    col = lax.broadcasted_iota(jnp.int32, (cols, LANES), 0)
    lane = lax.broadcasted_iota(jnp.int32, (cols, LANES), 1)
    slot = lax.broadcasted_iota(jnp.int32, (LANES, LANES), 0)
    slot_lane = lax.broadcasted_iota(jnp.int32, (LANES, LANES), 1)
    per = slots // groups
    f_here = g * members + me
    for layer in range(layers):
        rows = sum(all_ref[rank, layer, 8:16, :] for rank in range(members))
        gain = jnp.concatenate([rows[k : k + 1, :] for k in range(2)], axis=1)
        state2 = cols // 3
        shared = [rows[2 + k // 3 : 3 + k // 3, (k % 3) * state2 : (k % 3 + 1) * state2] for k in range(taps + 2)]
        skip = alog = 0.0
        for rank in range(members):
            start = col - (col >= span).astype(jnp.int32) * 0
            group = sum((start >= k * span).astype(jnp.int32) for k in range(1, groups))
            inside = start - group * span
            sub = sum((inside >= k * width).astype(jnp.int32) for k in range(1, per))
            hit = lane == (group * members + rank) * per + sub
            skip = skip + dot_high(
                all_ref[rank, layer, taps + 2 : taps + 3, :], jnp.where(hit, 1.0, 0.0)
            )
            group = sum((slot >= k * per).astype(jnp.int32) for k in range(1, groups))
            hit = (slot_lane == (group * members + rank) * per + slot - group * per) & (slot < slots)
            alog = alog + dot_high(
                all_ref[rank, layer, taps + 3 : taps + 4, :LANES], jnp.where(hit, 1.0, 0.0)
            )
        skip_out[layer : layer + 1, :] = skip[:, :heads]
        alog_out[layer : layer + 1, :] = alog[:, :heads]
        bias_out[layer : layer + 1, :] = shared[taps + 1][:, :heads]

        def blocks(first, size, row):
            pieces = []
            while size > 0:
                if first >= inner:
                    pieces.append(shared[row][:, first - inner : first - inner + size])
                    break
                block, off = first // span, first % span
                take = min(size, span - off)
                at = (block // members) * span + off
                pieces.append(all_ref[block % members, layer, row : row + 1, at : at + take])
                first, size = first + take, size - take
            return jnp.concatenate(pieces, axis=1) if len(pieces) > 1 else pieces[0]

        for f in range(groups * members):

            @pl.when(f_here == f)
            def _(f=f, layer=layer, gain=gain, blocks=blocks):
                norm_out[layer : layer + 1, :] = gain[:, f * rows_d : (f + 1) * rows_d]
                for k in range(taps):
                    taps_out[layer, k : k + 1, :] = blocks(f * conv_d, conv_d, k)
                conv_out[layer : layer + 1, :] = blocks(f * conv_d, conv_d, taps)
                gate_out[layer : layer + 1, :] = blocks(f * rows_i, rows_i, taps + 1)


def smem():
    return pl.BlockSpec(memory_space=pltpu.SMEM)


def vmem():
    return pl.BlockSpec(memory_space=pltpu.VMEM)


def call(body, outs, args, scalars=0, flops=0, scratch=(), name=None, spare=8):
    shapes = [jax.ShapeDtypeStruct(shape, dtype) for shape, dtype in outs]
    moved = sum(a.size * a.dtype.itemsize for a in args) + sum(
        s.size * s.dtype.itemsize for s in shapes
    )
    held = sum(np.prod(s.shape) * s.dtype.itemsize for s in scratch)
    single = len(shapes) == 1
    return pl.pallas_call(
        body,
        out_shape=shapes[0] if single else shapes,
        in_specs=[smem()] * scalars + [vmem()] * (len(args) - scalars),
        out_specs=vmem() if single else [vmem()] * len(shapes),
        scratch_shapes=list(scratch),
        cost_estimate=pl.CostEstimate(flops=flops, bytes_accessed=moved, transcendentals=0),
        compiler_params=pltpu.CompilerParams(
            vmem_limit_bytes=int(held * 5 // 4 + (spare << 20))
        ),
        name=name,
    )(*args)


class Plan:
    def __init__(self, mesh):
        self.fsdp = mesh.shape["fsdp"]
        self.rep = mesh.shape["rep"]
        self.members = INNER
        self.groups = self.fsdp // self.members
        self.ranks = self.members // 2 * self.rep

    def index(self, g, i, y):
        return (g * self.members + i) * self.rep + y

    def hop(self, x, move, only=None):
        pairs = []
        for g in range(self.groups):
            for i in range(self.members):
                for y in range(self.rep):
                    if only is None or only(g, i, y):
                        pairs.append((self.index(g, i, y), self.index(*move(g, i, y))))
        return lax.ppermute(x, AXES, pairs)

    def hop_c(self, x, only=None):
        return self.hop(x, lambda g, i, y: (g, i ^ 1, y), only)

    def hop_x(self, x):
        return self.hop(x, lambda g, i, y: (g, i ^ 2, y))

    def hop_y(self, x, only=None):
        return self.hop(x, lambda g, i, y: (g, i, y ^ 1), only)

    def hop_xy(self, x):
        return self.hop(x, lambda g, i, y: (g, i ^ 2, y ^ 1))

    def hop_xc(self, x):
        return self.hop(x, lambda g, i, y: (g, i ^ 3, y))

    def hop_cy(self, x, only=None):
        return self.hop(x, lambda g, i, y: (g, i ^ 1, y ^ 1), only)

    def hop_xcy(self, x):
        return self.hop(x, lambda g, i, y: (g, i ^ 3, y ^ 1))

    def hop_z(self, x):
        return self.hop(x, lambda g, i, y: ((g + 1) % self.groups, i, y))

    def hop_g(self, x, bit):
        return self.hop(x, lambda g, i, y: (g ^ bit, i, y))


def owner_core(g, i, y):
    return i % 2 == y


def other_core(g, i, y):
    return i % 2 != y


def after(x, *others):
    xs = list(x) if isinstance(x, (list, tuple)) else [x]
    held = list(lax.optimization_barrier(tuple(xs) + others)[: len(xs)])
    return held if isinstance(x, (list, tuple)) else held[0]


def ring_gather(plan, x):
    held = [x]
    for _ in range(1, plan.groups):
        x = plan.hop_z(x)
        held.append(x)
    return held


class Gathering:
    def __init__(self, plan, blocks):
        self.plan = plan
        self.held = [[x] for x in blocks]

    def step(self, *gates):
        if len(self.held[0]) < self.plan.groups:
            newest = after([part[-1] for part in self.held], *gates)
            for part, x in zip(self.held, newest):
                part.append(self.plan.hop_z(x))

    def newest(self):
        return [part[-1] for part in self.held]

    def finish(self, *gates):
        while len(self.held[0]) < self.plan.groups:
            self.step(*gates)
        return self.held


class Reducing:
    def __init__(self, plan, g, owns):
        self.plan, self.g, self.owns = plan, g, owns
        self.taken = 0
        self.totals = [own(lax.rem(g + plan.groups - 1, plan.groups)) for own in owns]

    def step(self, *gates):
        groups = self.plan.groups
        if self.taken < groups - 1:
            at = lax.rem(self.g + 2 * groups - 2 - self.taken, groups)
            self.taken += 1
            came = [self.plan.hop_z(total) for total in self.totals]
            if gates:
                came[-1] = after(came[-1], *gates)
            self.totals = [
                (x.astype(F32) + own(at).astype(F32)).astype(BF)
                for x, own in zip(came, self.owns)
            ]

    def finish(self):
        while self.taken < self.plan.groups - 1:
            self.step()
        return self.totals


def ring_reduce(plan, g, own):
    return Reducing(plan, g, [own]).finish()[0]


def spread_row(plan, pay):
    return [pay, plan.hop_x(pay), plan.hop_y(pay), plan.hop_xy(pay)]


def collect_row(plan, parts):
    return [parts[0], plan.hop_x(parts[1]), plan.hop_y(parts[2]), plan.hop_xy(parts[3])]


def pad_to(x, size, axis):
    pads = [(0, 0)] * x.ndim
    pads[axis] = (0, size - x.shape[axis])
    return jnp.pad(x, pads)


def pick(x, at, axis):
    return lax.dynamic_index_in_dim(x, at, axis, keepdims=False)


def local(
    plan,
    hidden_in,
    seg_ids,
    norm_gain,
    in_weight,
    conv_weight,
    conv_bias,
    dt_bias,
    a_log,
    d_skip,
    gate_gain,
    out_weight,
    cotangent,
):
    layers, rows_d, wide = in_weight.shape
    model = hidden_in.shape[1]
    tokens = seg_ids.shape[1]
    heads = dt_bias.shape[1]
    rows_i = out_weight.shape[1]
    inner = rows_i * plan.fsdp
    width = inner // heads
    conv_d = conv_bias.shape[1]
    state2 = conv_d * plan.fsdp - inner
    state = state2 // 2
    taps = conv_weight.shape[1]
    groups, members, reps, ranks = plan.groups, plan.members, plan.rep, plan.ranks
    slots = heads // ranks
    cols = slots * width
    half = cols // 2
    span = model // 2
    small_cols = state2 + heads
    small_wide = state2 + LANES
    fast = (
        rows_i % width == 0
        and reps == 2
        and rows_d % (16 * reps) == 0
        and (model // groups) % LANES == 0
    )
    slices = groups if fast else 1

    f = lax.axis_index("fsdp")
    y = lax.axis_index("rep")
    g, i = f // members, f % members
    far, core = i // 2, i % 2
    rank = far * reps + y
    if fast:
        per_dev = rows_i // width
        my_heads = (
            jnp.arange(groups)[:, None] * (members * per_dev)
            + rank * per_dev
            + jnp.arange(per_dev)[None]
        ).reshape(-1)
    else:
        my_heads = rank * slots + jnp.arange(slots)
    here = jnp.concatenate([jnp.stack([g, i, y, far, core]), my_heads]).astype(jnp.int32)

    def all_channels(x):
        return jnp.moveaxis(x, 0, -2).reshape(x.shape[1:-1] + (-1,))

    def pick_half(x, at, axis):
        low, high = jnp.split(x, 2, axis=axis)
        return jnp.where(at == 0, low, high)

    if fast:
        own_out = pick_half(out_weight, core, 2)
        came_out = plan.hop_c(pick_half(out_weight, 1 - core, 2), owner_core)
        own_out = jnp.where(core == y, own_out, came_out)

    def slow_weights(layer):
        w = lax.all_gather(in_weight[layer], "fsdp", axis=0, tiled=True)
        z, v = (lax.dynamic_slice_in_dim(w, k * inner + rank * cols, cols, 1) for k in range(2))
        own, other = jnp.where(core == 0, z, v), jnp.where(core == 0, v, z)
        w = lax.all_gather(out_weight[layer], "fsdp", axis=0, tiled=True)
        w = lax.dynamic_slice_in_dim(w, rank * cols, cols, 0)
        return (
            [own[:, :half], own[:, half:]]
            + [other[:, :half], other[:, half:]]
            + [pick_half(w, core, 1), pick_half(w, 1 - core, 1)]
        )

    def start_weights(layer, *gates):
        piece = jax.ShapeDtypeStruct((rows_d, cols), BF)
        picked = pl.pallas_call(
            functools.partial(pick_columns_kernel, groups, members, reps, (0, inner)),
            grid=(1,),
            out_shape=[piece] * members,
            in_specs=[smem(), pl.BlockSpec((1, rows_d, wide), lambda k: (layer, 0, 0))],
            out_specs=[pl.BlockSpec((rows_d, cols), lambda k: (0, 0))] * members,
            name="pick_columns",
        )(after(here, *gates), in_weight)
        pieces = [picked[0]] + [
            hop(x) for hop, x in zip((plan.hop_c, plan.hop_x, plan.hop_xc), picked[1:])
        ]
        shape = ((model // groups, half), BF)
        low, high = call(
            arrange_kernel, [shape, shape], [here] + pieces, scalars=1, name="arrange"
        )
        return Gathering(plan, [low, high, own_out[layer]])

    def end_weights(ring, *gates):
        own = ring.finish(*gates)
        other = [[plan.hop_c(x) for x in part] for part in own]
        return own[0] + own[1] + other[0] + other[1] + own[2] + other[2]

    vec_lines = taps + 3
    vec_pad = -(-layers * vec_lines // 16) * 16
    lines = []
    for layer in range(layers):
        lines.append(pad_to(conv_weight[layer], small_wide, 1))
        lines.append(pad_to(conv_bias[layer][None], small_wide, 1))
        lines.append(pad_to(gate_gain[layer][None], small_wide, 1))
        lines.append(pad_to(norm_gain[layer][None], small_wide, 1))
    vectors = pad_to(jnp.concatenate(lines, axis=0), vec_pad, 0)
    if fast:
        cut = rows_d // reps
        piece = lax.dynamic_slice(
            in_weight, (0, y * cut, wide - small_cols), (layers, cut, small_cols)
        )
        piece = pad_to(piece, small_wide, 2).reshape(layers * cut, small_wide)
        small_ring = ring_gather(plan, jnp.concatenate([piece, vectors], axis=0))
        ring = start_weights(0)
        begun = ring.held[0][0]
        ring.step(small_ring[-1])
        ring.step()
        held = jnp.stack(small_ring)
        near = spread_row(plan, held)
        near = near + [plan.hop_c(x) for x in near]
        placed = call(
            functools.partial(
                place_small_kernel,
                groups,
                members,
                reps,
                layers,
                taps,
                (conv_d, rows_i, rows_d),
            ),
            [((model, small_wide), BF)] * layers
            + [((1, model), F32)] * layers
            + [((8, state2), F32)] * layers
            + [((8, cols), F32)] * layers,
            [here] + near + [dt_bias],
            scalars=1,
            scratch=[pltpu.VMEM((plan.fsdp, vec_pad, small_wide), F32)],
            name="place_small",
        )
        w_small, gains, small_vecs, rank_vecs = (
            placed[k * layers : (k + 1) * layers] for k in range(4)
        )
    else:
        w_small = [
            pad_to(
                lax.all_gather(
                    in_weight[layer][:, wide - small_cols :], "fsdp", axis=0, tiled=True
                ),
                small_wide,
                1,
            )
            for layer in range(layers)
        ]
        vectors = lax.all_gather(vectors, "fsdp", axis=0)
        vectors = jnp.swapaxes(vectors.astype(F32), 0, 1)
        gains, small_vecs, rank_vecs = [], [], []
        for layer in range(layers):
            at = layer * vec_lines
            conv = vectors[at : at + taps + 1, :, :conv_d].reshape(taps + 1, -1)
            gate = vectors[at + taps + 1, :, :rows_i].reshape(1, -1)
            gains.append(vectors[at + taps + 2, :, :rows_d].reshape(1, -1))
            bias = pad_to(pad_to(dt_bias[layer][None], state2, 1), 8 - taps - 1, 0)
            small_vecs.append(jnp.concatenate([conv[:, inner:], bias], axis=0))
            own = jnp.concatenate([conv[:, :inner], gate], axis=0)
            own = lax.dynamic_slice_in_dim(own, rank * cols, cols, 1)
            rank_vecs.append(pad_to(own, 8, 0))

    seg_wide = jnp.broadcast_to(seg_ids[0].astype(F32)[:, None], (tokens, LANES))
    small_dims = (model, state2, heads, taps)
    rank_dims = (model, state, slots, width, taps, heads)
    pay_in = ((tokens, model + state2 + LANES), BF)
    pay_out = ((tokens, model + LANES), BF)
    small_out = ((tokens, small_wide), F32)
    stream_out = ((tokens, model), F32)
    scale_out = ((tokens, LANES), F32)
    pairs = (slice(0, 2), slice(2, 4))
    rows = 2
    block = rows * tokens
    flops = 2 * block * model * cols * 3
    side = state2 + LANES

    h = hidden_in
    streams, smalls, raws, scales, spreads, saved = [h], [], [], [], [], []
    pay, small = call(
        functools.partial(first_kernel, small_dims),
        [pay_in, small_out],
        [h, seg_wide, gains[0], w_small[0], small_vecs[0]],
        flops=2 * tokens * model * small_wide,
        name="first",
    )
    if fast:
        weights = [end_weights(ring, pay)]
        last, ring = ring.held[2][-1], None
        if layers > 1:
            ring = start_weights(1, begun)
            ring.step(last)
    else:
        weights = [slow_weights(layer) for layer in range(layers)]
        ring = None
    for layer in range(layers):
        smalls.append(small)
        chips = spread_row(plan, pay)
        spreads.append(chips)
        parts, kept = [], []
        for pair in pairs:
            done = call(
                functools.partial(rank_forward_kernel, rank_dims, rows, slices, layer),
                [pay_out] * rows + [((2, block, cols), F32), ((block, cols), F32)],
                [here, a_log, d_skip] + chips[pair] + weights[layer] + [rank_vecs[layer]],
                scalars=3,
                flops=flops,
                scratch=[
                    pltpu.VMEM((block, cols), BF),
                    pltpu.VMEM((2, cols, span), BF),
                    pltpu.VMEM((block, side), BF),
                    pltpu.VMEM((block, LANES), BF),
                ],
                name="rank_forward",
                spare=12,
            )
            parts += done[:rows]
            kept.append(done[rows:])
        saved.append(kept)
        parts = collect_row(plan, parts)
        if ring is not None:
            ring.step()
            parts = after(parts, *ring.newest())
        if layer + 1 < layers:
            pay, small, h, raw, scale = call(
                functools.partial(middle_kernel, small_dims, inner),
                [pay_in, small_out, stream_out, stream_out, scale_out],
                parts
                + [h, seg_wide, gains[layer + 1], w_small[layer + 1], small_vecs[layer + 1]],
                flops=2 * tokens * model * small_wide,
                name="middle",
            )
            streams.append(h)
            if ring is not None:
                weights.append(end_weights(ring, pay))
                last, ring = ring.held[2][-1], None
                if layer + 2 < layers:
                    ring = start_weights(layer + 2, pay)
                    ring.step(last)
        else:
            pay, h, raw, scale = call(
                functools.partial(turn_kernel, inner),
                [pay_out, stream_out, stream_out, scale_out],
                parts + [h, seg_wide, cotangent],
                name="turn",
            )
        raws.append(raw)
        scales.append(scale)
    stream = h

    def slow_reduce(keep, sent):
        z, v = jnp.where(core == 0, keep, sent), jnp.where(core == 0, sent, keep)
        full = jnp.zeros((model, 2, inner), F32)
        for k, part in enumerate((z, v)):
            full = lax.dynamic_update_slice(
                full, part[:model, None].astype(F32), (0, k, rank * cols)
            )
        full = lax.psum(full, "rep")
        grad_in = lax.psum_scatter(full, "fsdp", scatter_dimension=0, tiled=True)
        full = jnp.zeros((inner, model), F32)
        both = jnp.concatenate([z[model:], v[model:]], axis=1).astype(F32)
        full = lax.psum(lax.dynamic_update_slice(full, both, (rank * cols, 0)), "rep")
        grad_out = lax.psum_scatter(full, "fsdp", scatter_dimension=0, tiled=True)
        return grad_in.reshape(rows_d, 2 * inner), grad_out

    def start_reduce(keep, came, chunks, *more):
        def own(start, size, lane, wide):
            def at(b, row=0, count=size):
                spot = (start + b * size + row, lane)
                mine = lax.dynamic_slice(keep, spot, (count, wide))
                theirs = lax.dynamic_slice(came, spot, (count, wide))
                return (mine.astype(F32) + theirs.astype(F32)).astype(BF)

            return at

        wide = span // chunks
        owns = [own(0, model // groups, q * wide, wide) for q in range(chunks)]
        return Reducing(plan, g, [own(model, cols // groups, 0, span)] + owns + list(more))

    def exchange(total_out, *totals):
        chunks = []
        for total in totals:
            size = total.shape[0] // 2
            mine = lax.dynamic_slice_in_dim(total, far * size, size, 0)
            came = plan.hop_x(lax.dynamic_slice_in_dim(total, (1 - far) * size, size, 0))
            sent = [
                lax.dynamic_slice_in_dim(x, (1 - core) * rows_d, rows_d, 0) for x in (mine, came)
            ]
            kept = [lax.dynamic_slice_in_dim(x, core * rows_d, rows_d, 0) for x in (mine, came)]
            pieces = jnp.concatenate(kept + [plan.hop_c(jnp.concatenate(sent, axis=0))], axis=0)
            chunks.append([pieces, plan.hop_y(pieces)])
        both = jnp.concatenate([total_out, plan.hop_c(total_out, other_core)], axis=0)
        return chunks, [both, plan.hop_y(both, owner_core)]

    def slow_small(gw):
        return lax.psum_scatter(gw.astype(F32), "fsdp", scatter_dimension=0, tiled=True) / 2

    def small_block(gw):
        cut = rows_d // reps
        v = gw.reshape(groups, 2, 2, reps, cut, small_wide)
        v = pick(pick(v, y, 3), far, 1)
        mine = pick(v, core, 1)
        came = plan.hop_c(pick(v, 1 - core, 1))
        mine = (mine.astype(F32) + came.astype(F32)).astype(BF)
        return lambda b: pick(mine, b, 0)

    def spread_layer(layer, sofar):
        chunks, outs = grads_in[layer], grads_out[layer]
        args = [here] + [x for chunk in chunks for x in chunk] + small_grads[layer] + outs
        specs = [smem()] + [vmem()] * (len(args) - 1)
        shapes = ((layers, rows_d, wide), (layers, rows_i, model))
        alias = {}
        if sofar is not None:
            alias = {len(args): 0, len(args) + 1: 1}
            args = args + list(sofar)
            specs = specs + [pl.BlockSpec(memory_space=pl.ANY)] * 2
        return pl.pallas_call(
            functools.partial(
                spread_grads_kernel, groups, members, reps, (0, inner), len(chunks)
            ),
            grid=(1,),
            out_shape=[jax.ShapeDtypeStruct(shape, F32) for shape in shapes],
            in_specs=specs,
            out_specs=[
                pl.BlockSpec((1,) + shape[1:], lambda k, layer=layer: (layer, 0, 0))
                for shape in shapes
            ],
            input_output_aliases=alias,
            name="spread_grads",
        )(*args)

    grad = cotangent
    ring = sofar = None
    grads_in, grads_out, small_grads, vec_grads = {}, {}, {}, {}
    for layer in reversed(range(layers)):
        chips, cots = spreads[layer], spread_row(plan, pay)
        parts, gs_list, mixed_list, vec_list = [], [], [], []
        for pair, kept in zip(pairs, saved[layer]):
            if ring is not None:
                cots[pair] = after(cots[pair], *ring.totals)
                ring.step()
            done = call(
                functools.partial(rank_backward_kernel, rank_dims, rows, slices, layer),
                [pay_in] * rows
                + [((2, block, cols), BF), ((block, cols), BF), ((8, cols), F32)],
                [here, a_log, d_skip]
                + cots[pair]
                + chips[pair]
                + weights[layer]
                + [rank_vecs[layer]]
                + list(kept),
                scalars=3,
                flops=2 * flops,
                scratch=[
                    pltpu.VMEM((block, cols), F32),
                    pltpu.VMEM((tokens, tokens), F32),
                    pltpu.VMEM((tokens, cols), F32),
                    pltpu.VMEM((2, cols, span), BF),
                    pltpu.VMEM((block, side), BF),
                    pltpu.VMEM((block, LANES), BF),
                    pltpu.VMEM((block, side), BF),
                ],
                name="rank_backward",
                spare=16,
            )
            parts += done[:rows]
            gs_list.append(done[rows])
            mixed_list.append(done[rows + 1])
            vec_list.append(done[rows + 2])
        parts = collect_row(plan, parts)
        halves = [
            call(
                functools.partial(
                    weight_grad_kernel, flip, (len(chips), len(gs_list)), 2 * LANES
                ),
                [((model + cols, span), BF)],
                [here] + chips + gs_list + mixed_list + cots,
                scalars=1,
                flops=flops,
                name="weight_grad",
            )
            for flip in (True, False)
        ]
        if fast:
            halves[0] = plan.hop_c(halves[0])
        parts = after(parts, halves[1])
        done_ring = None
        if ring is not None:
            done_ring = ring.finish()
            parts = after(parts, *done_ring)
        more = layer > 0
        if fast and not more:
            ring = start_reduce(halves[1], halves[0], 2)
            ring.step()
            parts = after(parts, ring.totals[0])
        done = call(
            functools.partial(back_kernel, small_dims, inner, more),
            [stream_out, ((tokens, small_wide), BF), ((16, cols), F32)]
            + ([pay_out] if more else []),
            parts
            + [
                streams[layer],
                seg_wide,
                gains[layer],
                w_small[layer],
                small_vecs[layer],
                smalls[layer],
                grad,
            ]
            + vec_list
            + ([raws[layer - 1], scales[layer - 1]] if more else []),
            flops=2 * tokens * model * small_wide,
            name="back",
        )
        grad, gs, vec_grads[layer] = done[:3]
        if more:
            pay = done[3]
            halves = after(halves, pay)
        if done_ring is not None:
            done_ring = after(done_ring, gs)
            grads_in[layer + 1], grads_out[layer + 1] = exchange(*done_ring[:-1])
            small_grads[layer + 1] = [done_ring[-1], plan.hop_y(done_ring[-1])]
            sofar = spread_layer(layer + 1, sofar)
        near_gs = spread_row(plan, gs)
        if fast and not more:
            ring.step()
            near_gs = after(near_gs, ring.totals[0])
        small = call(
            functools.partial(small_grad_kernel, len(chips), 2 * LANES),
            [((model, small_wide), BF)],
            chips + near_gs,
            flops=2 * 2 * block * small_wide * model,
            name="small_grad",
        )
        if not fast:
            grads_in[layer], grads_out[layer] = slow_reduce(halves[1], halves[0])
            small_grads[layer] = slow_small(small)
        elif more:
            ring = start_reduce(halves[1], halves[0], 1, small_block(small))
            ring.step()
        else:
            total = ring_reduce(plan, g, small_block(small))
            small_grads[layer] = [total, plan.hop_y(total)]
            ring.step(*(sofar or ()))
            grads_in[layer], grads_out[layer] = exchange(*ring.finish())
            sofar = spread_layer(layer, sofar)

    if fast:
        grad_in, grad_out = sofar
    else:
        grad_in = jnp.stack(
            [
                jnp.concatenate([grads_in[l], small_grads[l][:, :small_cols]], axis=1)
                for l in range(layers)
            ]
        )
        grad_out = jnp.stack([grads_out[l] for l in range(layers)])

    vec = jnp.stack([vec_grads[l] for l in range(layers)])
    if fast:
        vec = vec + plan.hop_c(vec)
        bit = 1
        while bit < groups:
            vec = vec + plan.hop_g(vec, bit)
            bit *= 2
        norm_own, taps_own, conv_own, bias_sum, alog_sum, skip_sum, gate_own = (
            lambda o: (o[0], o[1], o[2], o[4], o[5], o[6], o[3])
        )(
            call(
                functools.partial(
                    spread_vectors_kernel, groups, members, reps, layers, taps, heads
                ),
                [
                    ((layers, rows_d), F32),
                    ((layers, taps, conv_d), F32),
                    ((layers, conv_d), F32),
                    ((layers, rows_i), F32),
                    ((layers, heads), F32),
                    ((layers, heads), F32),
                    ((layers, heads), F32),
                ],
                [here] + spread_row(plan, vec),
                scalars=1,
                scratch=[pltpu.VMEM((members,) + vec.shape, F32)],
                name="spread_vectors",
            )
        )
    else:
        full = jnp.zeros((ranks, layers, 8, cols), F32)
        full = lax.dynamic_update_slice(full, vec[None, :, :8], (rank, 0, 0, 0))
        by_rank = lax.psum(full, AXES)
        lines = lax.psum(vec[:, 8:], AXES)
        chan = all_channels(by_rank[:, :, : taps + 2])
        first, per = model // cols, cols // state2
        shared = [
            lines[:, first + k // per, (k % per) * state2 : (k % per + 1) * state2]
            for k in range(taps + 2)
        ]
        conv_all = jnp.concatenate(
            [chan[:, : taps + 1], jnp.stack(shared[: taps + 1], axis=1)], axis=-1
        )
        conv_own = lax.dynamic_slice_in_dim(conv_all, f * conv_d, conv_d, 2)
        taps_own, conv_own = conv_own[:, :taps], conv_own[:, taps]
        gate_own = lax.dynamic_slice_in_dim(chan[:, taps + 1], f * rows_i, rows_i, 1)
        norm_own = lax.dynamic_slice_in_dim(
            lines[:, :first].reshape(layers, model), f * rows_d, rows_d, 1
        )
        bias_sum = shared[taps + 1][:, :heads]
        skip_sum = all_channels(
            by_rank[:, :, taps + 2].reshape(ranks, layers, slots, width).sum(-1)
        )
        alog_sum = all_channels(by_rank[:, :, taps + 3, :slots])
    return (
        stream,
        grad,
        norm_own,
        grad_in,
        taps_own,
        conv_own,
        bias_sum,
        alog_sum,
        skip_sum,
        gate_own,
        grad_out,
    )


def solution(mesh):
    rows = P(("fsdp", "rep"), None)
    vector = P(None, "fsdp")
    matrix = P(None, "fsdp", None)
    taps = P(None, None, "fsdp")
    in_specs = (
        rows, rows, vector, matrix, taps, vector, P(), P(), P(), vector, matrix, rows,
    )
    out_specs = (
        rows, rows, vector, matrix, taps, vector, P(), P(), P(), vector, matrix,
    )
    return jax.shard_map(
        functools.partial(local, Plan(mesh)),
        mesh=mesh,
        in_specs=in_specs,
        out_specs=out_specs,
        check_vma=False,
    )
```
